32 devices in a mesh: gx: 8 (over z, core), gy: 4 (over y, x).
Axes of the slice: x: 2, y: 2, z: 4, core: 2. Of those that a mesh axis runs over, the one named last changes fastest.
Arguments:
- terminal: float32 [2048, 2048], P('gx', 'gy'), may hold values from -6 to 6
- crowding: float32 [2048, 2048], P('gx', 'gy'), may hold values from 0.5 to 4
- density: float32 [2048, 2048], P('gx', 'gy'), may hold values from 0.25 to 36, as said below
- fractions: float32 [4, 2, 2048, 2048], P(None, None, 'gx', 'gy'), may hold values from 0 to 1
- offsets: int32 [4, 8, 2], replicated, may hold values from -64 to 63
- control_cost: float32 [4, 8], replicated, may hold values from 0 to 4
Outputs:
- value_start: float32 [2048, 2048], P('gx', 'gy')
- density_end: float32 [2048, 2048], P('gx', 'gy')
- masses: float32 [4], replicated
The draws below stay inside these ranges and needn't reach their ends.
Inputs may be any that keep to these rules, and one draw needn't show every extreme that they name: `density`: positive.
All inputs are finite; a program needn't handle non-finite values.
Results may differ from the reference program's by a relative error of at most 0.0001.
Values sent between devices are 32-bit elements; how exact they have to be, the bound alone decides.
No kernel may reach another device: no remote copies, remote signals or barrier semaphores. Data moves between devices by JAX's collectives and lax.ppermute only.
A program may use at most 128 MiB of HBM per device.

```python
import math
from functools import reduce
import jax
import jax.numpy as jnp
from jax import lax

STEPS = 4
CONTROLS = 8
REACH = 64
NX = 2048
NY = 2048


def draw_density(key, part):
    first = jax.random.fold_in(jax.random.fold_in(key, 7), 0)
    rough = jnp.exp(jax.random.uniform(first, (NX, NY), jnp.float32, jnp.log(0.25), jnp.log(4.0)))
    row_place = jnp.arange(NX, dtype=jnp.float32) / NX
    profile = 1.0 + 2.0 * row_place[:, None] + jnp.zeros((NX, NY), jnp.float32)
    return jnp.clip(rough * profile, 0.25, 36.0)


def place_ends(values, rng, low, top_value):
    longest = values.shape.index(max(values.shape))
    spots = []
    for shift in (0, 1):
        where = [jax.random.randint(jax.random.fold_in(rng, axis), (), 0, length) for axis, length in enumerate(values.shape)]
        where[longest] = (where[longest] + shift) % values.shape[longest]
        spots.append(tuple(where))
    return values.at[spots[0]].set(low).at[spots[1]].set(top_value)


def steps_of(stream_key, dims, pieces, least, high):
    def one(position, blocks):
        heights = jax.random.uniform(jax.random.fold_in(jax.random.fold_in(stream_key, 6), position), (blocks,), jnp.float32, least / len(pieces), high / len(pieces))
        return jnp.repeat(jnp.exp(heights), dims[position] // blocks).reshape((-1,) + (1,) * (len(dims) - position - 1))

    level = one(*pieces[0])
    for cut in pieces[1:]:
        level = level * one(*cut)
    return level


def noise(stream_key, shape, spread, bound, cuts=(), kind=jnp.bfloat16):
    entries = jax.random.normal(stream_key, shape, jnp.float32) * spread
    if len(cuts) > 0:
        entries = steps_of(stream_key, shape, cuts, -0.22, 0.18) * entries
    return jnp.clip(entries, min=-bound, max=bound).astype(kind)


def setup_inputs(seed: int = 0) -> dict:
    arg_keys = jax.random.split(jax.random.key(seed), 7)
    terminal = noise(arg_keys[0], (NX, NY), 1.0, 6.0, ((0, 8), (1, 4)), jnp.float32)
    crowding = jnp.clip(jnp.exp(math.log(4.0) - 2.0794415 * jax.random.uniform(arg_keys[1], (NX, NY), jnp.float32) ** steps_of(arg_keys[1], (NX, NY), ((0, 8), (1, 4)), -0.2, 0.2)), 0.5, 4.0)
    density = draw_density(jax.random.fold_in(arg_keys[6], 71), 0)
    fractions = jnp.clip(1.0 * jax.random.uniform(arg_keys[3], (STEPS, 2, NX, NY), jnp.float32) ** steps_of(arg_keys[3], (STEPS, 2, NX, NY), ((2, 8), (3, 4)), -0.2, 0.2), 0.0, 1.0)
    offsets = place_ends(jax.random.randint(arg_keys[4], (STEPS, CONTROLS, 2), -REACH, REACH), jax.random.fold_in(arg_keys[4], 1), -REACH, REACH - 1).astype(jnp.int32)
    control_cost = jnp.clip(jax.random.uniform(arg_keys[5], (STEPS, CONTROLS), jnp.float32, 0.0, 4.0), 0.0, 4.0)
    return dict(terminal=terminal, crowding=crowding, density=density, fractions=fractions, offsets=offsets, control_cost=control_cost)


time_step = 0.1
temper = 0.3
epsilon = 1e-6


def catmull(fraction):
    square = fraction * fraction
    cube = square * fraction
    return [(-cube + 2.0 * square - fraction) * 0.5, (3.0 * cube - 5.0 * square + 2.0) * 0.5, (-3.0 * cube + 4.0 * square + fraction) * 0.5, (cube - square) * 0.5]


def sample(padded, weights_x, weights_y, shift_row, shift_col, margin, height, breadth):
    summed = None
    for row_tap in range(4):
        partial_sum = None
        for col_tap in range(4):
            piece = lax.dynamic_slice(padded, (margin + shift_row + row_tap - 1, margin + shift_col + col_tap - 1), (height, breadth))
            term = weights_y[col_tap] * piece
            partial_sum = term if partial_sum is None else partial_sum + term
        term = weights_x[row_tap] * partial_sum
        summed = term if summed is None else summed + term
    return summed


def option_values(padded, weights_x, weights_y, offsets, control_cost, crowding, moment, margin, height, breadth):
    candidates = []
    for option in range(offsets.shape[1]):
        shifted = sample(padded, weights_x, weights_y, offsets[moment, option, 0], offsets[moment, option, 1], margin, height, breadth)
        candidates.append(shifted + time_step * (control_cost[moment, option] + crowding))
    return candidates


def policy(candidates):
    lowest = reduce(jnp.minimum, candidates)
    ramps = [jnp.maximum(lowest + temper - candidate, 0.0) for candidate in candidates]
    ramp_sum = reduce(jnp.add, ramps)
    return lowest, [ramp / ramp_sum for ramp in ramps]


def reference(terminal, crowding, density, fractions, offsets, control_cost):
    margin = REACH + 2
    height, breadth = terminal.shape
    current_value = terminal
    policies = [None] * STEPS
    for moment in reversed(range(STEPS)):
        padded = jnp.pad(current_value, margin, mode="wrap")
        weights_x = catmull(fractions[moment, 0])
        weights_y = catmull(fractions[moment, 1])
        candidates = option_values(padded, weights_x, weights_y, offsets, control_cost, crowding, moment, margin, height, breadth)
        current_value, policies[moment] = policy(candidates)
    current = density
    mass_list = []
    for moment in range(STEPS):
        weights_x = catmull(fractions[moment, 0])
        weights_y = catmull(fractions[moment, 1])
        padded = jnp.pad(current, margin, mode="wrap")
        arrived = None
        for option in range(CONTROLS):
            shifted = sample(padded, weights_x, weights_y, -offsets[moment, option, 0], -offsets[moment, option, 1], margin, height, breadth)
            term = policies[moment][option] * shifted
            arrived = term if arrived is None else arrived + term
        arrived = jnp.maximum(arrived, 0.0)
        mean_mass = jnp.sum(arrived) / (NX * NY)
        mass_list.append(mean_mass)
        current = arrived / (mean_mass + epsilon)
    return current_value, current, jnp.stack(mass_list)
```

```python
import functools

import jax
import jax.numpy as jnp
from jax import lax
from jax.experimental import pallas as pl
from jax.experimental.pallas import tpu as pltpu
from jax.sharding import PartitionSpec as P

REACH = 64
LANES = 128
SUBLANES = 8
TAPS = 4
FIELDS = 3 * TAPS
ROW_HALO = -(-(REACH + 2) // SUBLANES) * SUBLANES

time_step = 0.1
temper = 0.3
epsilon = 1e-06


def catmull(fraction):
    square = fraction * fraction
    cube = square * fraction
    return [
        (-cube + 2.0 * square - fraction) * 0.5,
        (3.0 * cube - 5.0 * square + 2.0) * 0.5,
        (-3.0 * cube + 4.0 * square + fraction) * 0.5,
        (cube - square) * 0.5,
    ]


def shift_table(offsets, padded_rows):
    taps = jnp.arange(TAPS, dtype=jnp.int32) - 1
    tables = []
    for sign in (1, -1):
        move = sign * offsets[..., 1:] + taps
        around = jnp.where(move < 0, move + LANES, move)
        row = ROW_HALO - 1 + sign * offsets[..., :1] + jnp.where(move < 0, 0, padded_rows)
        tables.append(jnp.concatenate([row, (LANES - around) % LANES, LANES - around], axis=-1))
    return jnp.stack(tables).astype(jnp.int32).reshape(-1)


def stage(tiles, top, bottom, left, right, padded):
    height = tiles[0].shape[0]
    count = len(tiles)
    pitch = padded.shape[0] // (count + 2)
    for tile in range(count):
        at = (tile + 1) * pitch
        padded[at : at + ROW_HALO, :] = top[tile]
        padded[at + ROW_HALO : at + ROW_HALO + height, :] = tiles[tile][...]
        padded[at + ROW_HALO + height : at + 2 * ROW_HALO + height, :] = bottom[tile]
    if left is not None:
        at = (count + 1) * pitch
        padded[0 : 2 * ROW_HALO + height, :] = left[...]
        padded[at : at + 2 * ROW_HALO + height, :] = right[...]


def shift_block(table, entry, pairs, wanted, block, pitch, padded, cuts, shifted):
    start = pl.multiple_of(block * SUBLANES, SUBLANES)
    for k, tap in pairs:
        at = entry + k * FIELDS + tap
        row = table[at] + start
        turn = table[at + TAPS]
        keep = cuts[k * TAPS + tap] > 0
        turned = {}
        for tile in wanted:
            for part in (tile, tile + 1):
                if part not in turned:
                    turned[part] = pltpu.roll(padded[pl.ds(row + part * pitch, SUBLANES), :], turn, 1)
        for n, tile in enumerate(wanted):
            shifted[k, n, tap, pl.ds(start, SUBLANES), :] = jnp.where(keep, turned[tile], turned[tile + 1])


def interpolate(shifted, k, n, start, weights):
    summed = None
    for row_tap in range(TAPS):
        partial_sum = None
        for col_tap in range(TAPS):
            piece = shifted[k, n, col_tap, pl.ds(start + row_tap, SUBLANES), :]
            term = weights[row_tap][col_tap] * piece
            partial_sum = term if partial_sum is None else partial_sum + term
        summed = partial_sum if summed is None else summed + partial_sum
    return summed


def products(fraction, here):
    weights_x = catmull(fraction[0, 0, here, :])
    weights_y = catmull(fraction[0, 1, here, :])
    return [[x * y for y in weights_y] for x in weights_x]


def sweep(table, entry, wanted, rows, pitch, padded, cuts, shifted, finish, carry):
    controls = shifted.shape[0]
    chunk = pl.program_id(0)
    first = chunk * (rows // SUBLANES)
    blocks = shifted.shape[3] // SUBLANES
    pairs = [(k, tap) for k in range(controls) for tap in range(TAPS)]

    @pl.when(chunk == 0)
    def _():
        lane = lax.broadcasted_iota(jnp.int32, (SUBLANES, LANES), 1)
        for k, tap in pairs:
            cuts[k * TAPS + tap] = table[entry + k * FIELDS + 2 * TAPS + tap] - lane

        def ahead(block, nothing):
            shift_block(table, entry, pairs, wanted, block, pitch, padded, cuts, shifted)
            return nothing

        lax.fori_loop(0, blocks, ahead, 0, unroll=3 if blocks % 3 == 0 else 1)

    def one_block(block, carry):
        start = pl.multiple_of((first + block) * SUBLANES, SUBLANES)
        here = pl.ds(pl.multiple_of(block * SUBLANES, SUBLANES), SUBLANES)
        for n in range(len(wanted)):

            def sampled(k, weights):
                return interpolate(shifted, k, n, start, weights)

            carry = finish(n, start, here, sampled, carry)
        return carry

    return lax.fori_loop(0, rows // SUBLANES, one_block, carry)


def edges_out(values, inner_top, inner_bottom, top, bottom):
    height = values[0].shape[0]
    if inner_top is None:
        for n in range(len(values)):
            top[n] = values[n][0:ROW_HALO, :]
            bottom[n] = values[n][height - ROW_HALO : height, :]
        return
    count = top.shape[0]
    for n, tile in enumerate((0, count - 1)):
        top[tile] = values[n][0:ROW_HALO, :]
        bottom[tile] = values[n][height - ROW_HALO : height, :]
    for tile in range(1, count - 1):
        top[tile] = inner_top[tile - 1]
        bottom[tile] = inner_bottom[tile - 1]


def step_kernel(wanted, count, moment_entry, cost_entry, rows, is_backward, is_outer, *refs):
    refs = list(refs)
    take = lambda n: [refs.pop(0) for _ in range(n)]
    (table,) = take(1)
    costs = take(1)[0] if is_backward else None
    tiles = take(count)
    top, bottom = take(2)
    left, right, inner_top, inner_bottom = take(4) if is_outer else (None,) * 4
    fractions = take(len(wanted))
    if is_backward:
        crowding = take(len(wanted))
    else:
        ramps, inverse = take(2)
    values = take(len(wanted))
    edge_top, edge_bottom = take(2)
    if is_backward:
        ramps, inverse = take(2)
    else:
        (mass,) = take(1)
    padded, cuts, shifted = take(3)
    pitch = padded.shape[0] // (count + 2)
    controls = shifted.shape[0]

    @pl.when(pl.program_id(0) == 0)
    def _():
        stage(tiles, top, bottom, left, right, padded)
        if not is_backward:
            mass[...] = jnp.zeros_like(mass)

    def finish_backward(n, start, here, sampled, carry):
        weights = products(fractions[n], here)
        candidates = [sampled(k, weights) + costs[cost_entry + k] for k in range(controls)]
        lowest = functools.reduce(jnp.minimum, candidates)
        values[n][pl.ds(start, SUBLANES), :] = lowest + time_step * crowding[n][here, :]
        level = lowest + temper
        total = None
        for k in range(controls):
            ramp = jnp.maximum(level - candidates[k], 0.0)
            ramps[n, k, here, :] = ramp
            total = ramp if total is None else total + ramp
        inverse[n, here, :] = 1.0 / total
        return carry

    def finish_forward(n, start, here, sampled, sums):
        weights = products(fractions[n], here)
        total = None
        for k in range(controls):
            term = ramps[n, k, here, :] * sampled(k, weights)
            total = term if total is None else total + term
        total = jnp.maximum(total * inverse[n, here, :], 0.0)
        values[n][pl.ds(start, SUBLANES), :] = total
        return sums + total

    if is_backward:
        sweep(table, moment_entry, wanted, rows, pitch, padded, cuts, shifted, finish_backward, 0)
    else:
        zero = jnp.zeros((SUBLANES, LANES), jnp.float32)
        mass[...] += sweep(table, moment_entry, wanted, rows, pitch, padded, cuts, shifted, finish_forward, zero)

    @pl.when(pl.program_id(0) == pl.num_programs(0) - 1)
    def _():
        edges_out(values, inner_top, inner_bottom, edge_top, edge_bottom)


def padded_rows(height):
    return height + 2 * ROW_HALO + SUBLANES


def row_chunk(height):
    for rows in (64, 32, 16, 8):
        if height % rows == 0:
            return rows
    return height


def step(wanted, entry, cost_entry, controls, moment, table, tiles, halo, sides, inner, fractions, backward, forward):
    is_backward, is_outer = backward is not None, sides is not None
    height = tiles[0].shape[0]
    count = len(tiles)
    group = len(wanted)
    rows = row_chunk(height)
    whole = lambda *shape: pl.BlockSpec(shape, lambda c: (0,) * len(shape))
    smem = pl.BlockSpec(memory_space=pltpu.SMEM)
    edge = whole(count, ROW_HALO, LANES)
    inner_edge = whole(count - 2, ROW_HALO, LANES)
    fraction = [
        pl.BlockSpec((1, 2, rows, LANES), functools.partial(lambda t, c: (moment, 0, c, t), tile)) for tile in wanted
    ]
    ramp = pl.BlockSpec((group, controls, rows, LANES), lambda c: (0, 0, c, 0))
    inverse = pl.BlockSpec((group, rows, LANES), lambda c: (0, c, 0))
    f32 = lambda *shape: jax.ShapeDtypeStruct(shape, jnp.float32)

    args, specs = [table], [smem]
    if is_backward:
        args, specs = args + [backward[0]], specs + [smem]
    args += [*tiles, *halo]
    specs += [whole(height, LANES)] * count + [edge] * 2
    if is_outer:
        args += [*sides, *inner]
        specs += [whole(height + 2 * ROW_HALO, LANES)] * 2 + [inner_edge] * 2
    args += [fractions] * group
    specs += fraction
    if is_backward:
        args += [backward[1]] * group
        specs += [pl.BlockSpec((rows, LANES), functools.partial(lambda t, c: (c, t), tile)) for tile in wanted]
    else:
        args += [*forward]
        specs += [ramp, inverse]

    edge_count = count if is_outer else group
    outs = [f32(height, LANES)] * group + [f32(edge_count, ROW_HALO, LANES)] * 2
    out_specs = [whole(height, LANES)] * group + [whole(edge_count, ROW_HALO, LANES)] * 2
    if is_backward:
        outs += [f32(group, controls, height, LANES), f32(group, height, LANES)]
        out_specs += [ramp, inverse]
    else:
        outs += [f32(SUBLANES, LANES)]
        out_specs += [whole(SUBLANES, LANES)]
    results = pl.pallas_call(
        functools.partial(step_kernel, wanted, count, entry, cost_entry, rows, is_backward, is_outer),
        grid=(height // rows,),
        in_specs=specs,
        out_specs=out_specs,
        out_shape=outs,
        scratch_shapes=[
            pltpu.VMEM(((count + 2) * padded_rows(height), LANES), jnp.float32),
            pltpu.VMEM((controls * TAPS, SUBLANES, LANES), jnp.int32),
            pltpu.VMEM((controls, group, TAPS, height + SUBLANES, LANES), jnp.float32),
        ],
        cost_estimate=pl.CostEstimate(
            flops=64 * controls * group * height * LANES,
            bytes_accessed=4 * (controls + 6) * group * height * LANES,
            transcendentals=0,
        ),
        name=("backward" if is_backward else "forward") + ("_outer" if is_outer else "_inner"),
    )(*args)
    return results[:group], results[group : group + 2], results[group + 2 :]


def split_kernel(cells, *outs):
    *tiles, top, bottom = outs
    height = cells.shape[0]
    for n, tile in enumerate(tiles):
        piece = cells[:, n * LANES : (n + 1) * LANES]
        tile[...] = piece
        top[n] = piece[0:ROW_HALO, :]
        bottom[n] = piece[height - ROW_HALO : height, :]


def split(cells):
    height, breadth = cells.shape
    count = breadth // LANES
    f32 = lambda *shape: jax.ShapeDtypeStruct(shape, jnp.float32)
    results = pl.pallas_call(
        split_kernel,
        out_shape=[f32(height, LANES)] * count + [f32(count, ROW_HALO, LANES)] * 2,
        name="split",
    )(cells)
    return results[:count], results[count:]


def columns_kernel(top, bottom, first, last, first_out, last_out):
    height = first.shape[0]
    for tile, cells, out in ((0, first, first_out), (top.shape[0] - 1, last, last_out)):
        out[0:ROW_HALO, :] = top[tile]
        out[ROW_HALO : ROW_HALO + height, :] = cells[...]
        out[ROW_HALO + height : 2 * ROW_HALO + height, :] = bottom[tile]


def columns(halo, first, last):
    out = jax.ShapeDtypeStruct((first.shape[0] + 2 * ROW_HALO, LANES), jnp.float32)
    return pl.pallas_call(columns_kernel, out_shape=[out, out], name="columns")(*halo, first, last)


def passed(cells, axis, distance):
    count = lax.axis_size(axis)
    return lax.ppermute(cells, axis, [(i, (i + distance) % count) for i in range(count)])


def row_halo(edges):
    return passed(edges[1], "gx", 1), passed(edges[0], "gx", -1)


def column_halo(halo, tiles):
    first, last = columns(halo, tiles[0], tiles[-1])
    return passed(last, "gy", 1), passed(first, "gy", -1)


def everywhere(sums):
    for axis in ("gy", "gx"):
        count = lax.axis_size(axis)
        if count & (count - 1):
            sums = lax.psum(sums, axis)
            continue
        distance = 1
        while distance < count:
            sums = sums + lax.ppermute(sums, axis, [(i, i ^ distance) for i in range(count)])
            distance *= 2
    return sums


def shards(terminal, crowding, density, fractions, offsets, control_cost):
    height, breadth = terminal.shape
    count = breadth // LANES
    steps_count, controls = control_cost.shape
    cells = height * breadth * lax.axis_size("gx") * lax.axis_size("gy")
    table = shift_table(offsets, padded_rows(height))
    costs = time_step * control_cost.reshape(-1)
    inside, outside = tuple(range(1, count - 1)), (0, count - 1)

    def both_groups(tiles, halo, entry, moment, backward, policy):
        sides = column_halo(halo, tiles)
        common = (entry, moment * controls, controls, moment, table, tiles, halo)
        inner, inner_edges, inner_rest = step(
            inside, *common, None, None, fractions, backward, None if policy is None else policy[0]
        )
        outer, edges, outer_rest = step(
            outside, *common, sides, inner_edges, fractions, backward, None if policy is None else policy[1]
        )
        return [outer[0], *inner, outer[1]], edges, (inner_rest, outer_rest)

    tiles, edges = split(terminal)
    policies = [None] * steps_count
    for moment in reversed(range(steps_count)):
        entry = moment * controls * FIELDS
        tiles, edges, policies[moment] = both_groups(
            tiles, row_halo(edges), entry, moment, (costs, crowding), None
        )
    value = jnp.concatenate(tiles, axis=1)

    tiles, edges = split(density)
    local_sums = []
    for moment in range(steps_count):
        entry = (steps_count + moment) * controls * FIELDS
        tiles, edges, ((inner_mass,), (outer_mass,)) = both_groups(
            tiles, row_halo(edges), entry, moment, None, policies[moment]
        )
        local_sums.append(jnp.sum(inner_mass + outer_mass))
    totals = everywhere(jnp.stack(local_sums)) / cells
    masses = []
    scale = jnp.float32(1.0)
    for moment in range(steps_count):
        masses.append(totals[moment] / scale)
        scale = totals[moment] + epsilon * scale
    return (value, jnp.concatenate(tiles, axis=1) / scale, jnp.stack(masses))


def solution(mesh):
    return jax.shard_map(
        shards,
        mesh=mesh,
        in_specs=(P("gx", "gy"), P("gx", "gy"), P("gx", "gy"), P(None, None, "gx", "gy"), P(), P()),
        out_specs=(P("gx", "gy"), P("gx", "gy"), P()),
        check_vma=False,
    )
```

```python
import functools

import jax
import jax.numpy as jnp
from jax import lax
from jax.experimental import pallas as pl
from jax.experimental.pallas import tpu as pltpu
from jax.sharding import PartitionSpec as P

REACH = 64
LANES = 128
SUBLANES = 8
TAPS = 4
FIELDS = 3 * TAPS
ROW_HALO = -(-(REACH + 2) // SUBLANES) * SUBLANES

time_step = 0.1
temper = 0.3
epsilon = 1e-06


def catmull(fraction):
    square = fraction * fraction
    cube = square * fraction
    return [
        (-cube + 2.0 * square - fraction) * 0.5,
        (3.0 * cube - 5.0 * square + 2.0) * 0.5,
        (-3.0 * cube + 4.0 * square + fraction) * 0.5,
        (cube - square) * 0.5,
    ]


def shift_table(offsets, padded_rows):
    taps = jnp.arange(TAPS, dtype=jnp.int32) - 1
    tables = []
    for sign in (1, -1):
        move = sign * offsets[..., 1:] + taps
        around = jnp.where(move < 0, move + LANES, move)
        row = ROW_HALO - 1 + sign * offsets[..., :1] + jnp.where(move < 0, 0, padded_rows)
        tables.append(jnp.concatenate([row, (LANES - around) % LANES, LANES - around], axis=-1))
    return jnp.stack(tables).astype(jnp.int32).reshape(-1)


def stage(tiles, top, bottom, left, right, padded):
    height = tiles[0].shape[0]
    count = len(tiles)
    pitch = padded.shape[0] // (count + 2)
    for tile in range(count):
        at = (tile + 1) * pitch
        padded[at : at + ROW_HALO, :] = top[tile]
        padded[at + ROW_HALO : at + ROW_HALO + height, :] = tiles[tile][...]
        padded[at + ROW_HALO + height : at + 2 * ROW_HALO + height, :] = bottom[tile]
    if left is not None:
        at = (count + 1) * pitch
        padded[0 : 2 * ROW_HALO + height, :] = left[...]
        padded[at : at + 2 * ROW_HALO + height, :] = right[...]


def shift_block(table, entry, pairs, wanted, block, pitch, padded, cuts, shifted):
    start = pl.multiple_of(block * SUBLANES, SUBLANES)
    for k, tap in pairs:
        at = entry + k * FIELDS + tap
        row = table[at] + start
        turn = table[at + TAPS]
        keep = cuts[k * TAPS + tap] > 0
        turned = {}
        for tile in wanted:
            for part in (tile, tile + 1):
                if part not in turned:
                    turned[part] = pltpu.roll(padded[pl.ds(row + part * pitch, SUBLANES), :], turn, 1)
        for n, tile in enumerate(wanted):
            shifted[k, n, tap, pl.ds(start, SUBLANES), :] = jnp.where(keep, turned[tile], turned[tile + 1])


def interpolate(shifted, k, n, start, weights):
    summed = None
    for row_tap in range(TAPS):
        partial_sum = None
        for col_tap in range(TAPS):
            piece = shifted[k, n, col_tap, pl.ds(start + row_tap, SUBLANES), :]
            term = weights[row_tap][col_tap] * piece
            partial_sum = term if partial_sum is None else partial_sum + term
        summed = partial_sum if summed is None else summed + partial_sum
    return summed


def products(fraction, here):
    weights_x = catmull(fraction[0, 0, here, :])
    weights_y = catmull(fraction[0, 1, here, :])
    return [[x * y for y in weights_y] for x in weights_x]


def sweep(table, entry, wanted, rows, pitch, padded, cuts, shifted, finish, carry):
    controls = shifted.shape[0]
    chunk = pl.program_id(0)
    first = chunk * (rows // SUBLANES)
    blocks = shifted.shape[3] // SUBLANES
    pairs = [(k, tap) for k in range(controls) for tap in range(TAPS)]

    @pl.when(chunk == 0)
    def _():
        lane = lax.broadcasted_iota(jnp.int32, (SUBLANES, LANES), 1)
        for k, tap in pairs:
            cuts[k * TAPS + tap] = table[entry + k * FIELDS + 2 * TAPS + tap] - lane

        def ahead(block, nothing):
            shift_block(table, entry, pairs, wanted, block, pitch, padded, cuts, shifted)
            return nothing

        lax.fori_loop(0, blocks, ahead, 0, unroll=3 if blocks % 3 == 0 else 1)

    def one_block(block, carry):
        start = pl.multiple_of((first + block) * SUBLANES, SUBLANES)
        here = pl.ds(pl.multiple_of(block * SUBLANES, SUBLANES), SUBLANES)
        for n in range(len(wanted)):

            def sampled(k, weights):
                return interpolate(shifted, k, n, start, weights)

            carry = finish(n, start, here, sampled, carry)
        return carry

    return lax.fori_loop(0, rows // SUBLANES, one_block, carry)


def edges_out(values, inner_top, inner_bottom, top, bottom):
    height = values[0].shape[0]
    if inner_top is None:
        for n in range(len(values)):
            top[n] = values[n][0:ROW_HALO, :]
            bottom[n] = values[n][height - ROW_HALO : height, :]
        return
    count = top.shape[0]
    for n, tile in enumerate((0, count - 1)):
        top[tile] = values[n][0:ROW_HALO, :]
        bottom[tile] = values[n][height - ROW_HALO : height, :]
    for tile in range(1, count - 1):
        top[tile] = inner_top[tile - 1]
        bottom[tile] = inner_bottom[tile - 1]


def step_kernel(wanted, count, moment_entry, cost_entry, moment, rows, is_backward, is_outer, *refs):
    refs = list(refs)
    take = lambda n: [refs.pop(0) for _ in range(n)]
    (table,) = take(1)
    costs = take(1)[0] if is_backward else None
    tiles = take(count)
    top, bottom = take(2)
    left, right, inner_top, inner_bottom = take(4) if is_outer else (None,) * 4
    fractions = take(len(wanted))
    if is_backward:
        crowding = take(len(wanted))
    else:
        ramps, inverse = take(2)
        earlier, inner_mass = take(2) if is_outer else (None, None)
    values = take(len(wanted))
    edge_top, edge_bottom = take(2)
    if is_backward:
        ramps, inverse = take(2)
    else:
        (mass,) = take(1)
    padded, cuts, shifted = take(3)
    pitch = padded.shape[0] // (count + 2)
    controls = shifted.shape[0]

    @pl.when(pl.program_id(0) == 0)
    def _():
        stage(tiles, top, bottom, left, right, padded)
        if not is_backward:
            mass[...] = jnp.zeros_like(mass)

    def finish_backward(n, start, here, sampled, carry):
        weights = products(fractions[n], here)
        candidates = [sampled(k, weights) + costs[cost_entry + k] for k in range(controls)]
        lowest = functools.reduce(jnp.minimum, candidates)
        values[n][pl.ds(start, SUBLANES), :] = lowest + time_step * crowding[n][here, :]
        level = lowest + temper
        total = None
        for k in range(controls):
            ramp = jnp.maximum(level - candidates[k], 0.0)
            ramps[n, k, here, :] = ramp
            total = ramp if total is None else total + ramp
        inverse[n, here, :] = 1.0 / total
        return carry

    def finish_forward(n, start, here, sampled, sums):
        weights = products(fractions[n], here)
        total = None
        for k in range(controls):
            term = ramps[n, k, here, :] * sampled(k, weights)
            total = term if total is None else total + term
        total = jnp.maximum(total * inverse[n, here, :], 0.0)
        values[n][pl.ds(start, SUBLANES), :] = total
        return sums + total

    if is_backward:
        sweep(table, moment_entry, wanted, rows, pitch, padded, cuts, shifted, finish_backward, 0)
    else:
        zero = jnp.zeros((SUBLANES, LANES), jnp.float32)
        mass[...] += sweep(table, moment_entry, wanted, rows, pitch, padded, cuts, shifted, finish_forward, zero)

    @pl.when(pl.program_id(0) == pl.num_programs(0) - 1)
    def _():
        edges_out(values, inner_top, inner_bottom, edge_top, edge_bottom)
        if is_outer and not is_backward:
            place = lax.broadcasted_iota(jnp.int32, (SUBLANES, LANES), 0) * LANES
            place += lax.broadcasted_iota(jnp.int32, (SUBLANES, LANES), 1)
            mass[...] = jnp.where(place == moment, jnp.sum(mass[...] + inner_mass[...]), earlier[...])


def padded_rows(height):
    return height + 2 * ROW_HALO + SUBLANES


def row_chunk(height):
    for rows in (64, 32, 16, 8):
        if height % rows == 0:
            return rows
    return height


def step(wanted, entry, cost_entry, controls, moment, table, tiles, halo, sides, inner, fractions, backward, forward, which, sums):
    is_backward, is_outer = backward is not None, sides is not None
    height = tiles[0].shape[0]
    count = len(tiles)
    group = len(wanted)
    rows = row_chunk(height)
    whole = lambda *shape: pl.BlockSpec(shape, lambda c: (0,) * len(shape))
    smem = pl.BlockSpec(memory_space=pltpu.SMEM)
    edge = pl.BlockSpec((count, ROW_HALO, LANES), lambda c: (which, 0, 0))
    inner_edge = whole(count - 2, ROW_HALO, LANES)
    fraction = [
        pl.BlockSpec((1, 2, rows, LANES), functools.partial(lambda t, c: (moment, 0, c, t), tile)) for tile in wanted
    ]
    ramp = pl.BlockSpec((group, controls, rows, LANES), lambda c: (0, 0, c, 0))
    inverse = pl.BlockSpec((group, rows, LANES), lambda c: (0, c, 0))
    f32 = lambda *shape: jax.ShapeDtypeStruct(shape, jnp.float32)

    args, specs = [table], [smem]
    if is_backward:
        args, specs = args + [backward[0]], specs + [smem]
    args += [*tiles, *halo]
    specs += [whole(height, LANES)] * count + [edge] * 2
    if is_outer:
        args += [*sides, *inner]
        specs += [whole(height + 2 * ROW_HALO, LANES)] * 2 + [inner_edge] * 2
    args += [fractions] * group
    specs += fraction
    if is_backward:
        args += [backward[1]] * group
        specs += [pl.BlockSpec((rows, LANES), functools.partial(lambda t, c: (c, t), tile)) for tile in wanted]
    else:
        args += [*forward]
        specs += [ramp, inverse]
        if is_outer:
            args += [*sums]
            specs += [whole(SUBLANES, LANES)] * 2

    edge_count = count if is_outer else group
    outs = [f32(height, LANES)] * group + [f32(edge_count, ROW_HALO, LANES)] * 2
    out_specs = [whole(height, LANES)] * group + [whole(edge_count, ROW_HALO, LANES)] * 2
    if is_backward:
        outs += [f32(group, controls, height, LANES), f32(group, height, LANES)]
        out_specs += [ramp, inverse]
    else:
        outs += [f32(SUBLANES, LANES)]
        out_specs += [whole(SUBLANES, LANES)]
    results = pl.pallas_call(
        functools.partial(step_kernel, wanted, count, entry, cost_entry, moment, rows, is_backward, is_outer),
        grid=(height // rows,),
        in_specs=specs,
        out_specs=out_specs,
        out_shape=outs,
        scratch_shapes=[
            pltpu.VMEM(((count + 2) * padded_rows(height), LANES), jnp.float32),
            pltpu.VMEM((controls * TAPS, SUBLANES, LANES), jnp.int32),
            pltpu.VMEM((controls, group, TAPS, height + SUBLANES, LANES), jnp.float32),
        ],
        cost_estimate=pl.CostEstimate(
            flops=64 * controls * group * height * LANES,
            bytes_accessed=4 * (controls + 6) * group * height * LANES,
            transcendentals=0,
        ),
        name=("backward" if is_backward else "forward") + ("_outer" if is_outer else "_inner"),
    )(*args)
    return results[:group], results[group : group + 2], results[group + 2 :]


def split_kernel(fields, *refs):
    cells, tiles, (top, bottom) = refs[:fields], refs[fields:-2], refs[-2:]
    height = cells[0].shape[0]
    for n, tile in enumerate(tiles):
        field, column = divmod(n, len(tiles) // fields)
        piece = cells[field][:, column * LANES : (column + 1) * LANES]
        tile[...] = piece
        top[n] = piece[0:ROW_HALO, :]
        bottom[n] = piece[height - ROW_HALO : height, :]


def split(*fields):
    height, breadth = fields[0].shape
    count = breadth // LANES
    f32 = lambda *shape: jax.ShapeDtypeStruct(shape, jnp.float32)
    results = pl.pallas_call(
        functools.partial(split_kernel, len(fields)),
        out_shape=[f32(height, LANES)] * (count * len(fields)) + [f32(count * len(fields), ROW_HALO, LANES)] * 2,
        name="split",
    )(*fields)
    return [results[n * count : (n + 1) * count] for n in range(len(fields))], results[-2:]


def columns_kernel(places, top, bottom, first, last, first_out, last_out, ready):
    height = first.shape[0]
    copies = []
    for place, tile, out in zip(places, (first, last), (first_out, last_out)):
        parts = ((top.at[place], 0, ROW_HALO), (tile, ROW_HALO, height), (bottom.at[place], ROW_HALO + height, ROW_HALO))
        for source, start, rows in parts:
            copies.append(pltpu.make_async_copy(source, out.at[pl.ds(start, rows), :], ready.at[len(copies)]))
    for copy in copies:
        copy.start()
    for copy in copies:
        copy.wait()


def columns(halo, tiles, which):
    places = (which * len(tiles), which * len(tiles) + len(tiles) - 1)
    out = jax.ShapeDtypeStruct((tiles[0].shape[0] + 2 * ROW_HALO, LANES), jnp.float32)
    return pl.pallas_call(
        functools.partial(columns_kernel, places),
        in_specs=[pl.BlockSpec(memory_space=pl.ANY)] * 4,
        out_shape=[out, out],
        scratch_shapes=[pltpu.SemaphoreType.DMA((6,))],
        name="columns",
    )(*halo, tiles[0], tiles[-1])


def passed(cells, axis, distance):
    count = lax.axis_size(axis)
    return lax.ppermute(cells, axis, [(i, (i + distance) % count) for i in range(count)])


def row_halo(edges):
    return passed(edges[1], "gx", 1), passed(edges[0], "gx", -1)


def column_halo(halo, tiles, which=0):
    first, last = columns(halo, tiles, which)
    return passed(last, "gy", 1), passed(first, "gy", -1)


def everywhere(sums):
    for axis in ("gy", "gx"):
        count = lax.axis_size(axis)
        if count & (count - 1):
            sums = lax.psum(sums, axis)
            continue
        distance = 1
        while distance < count:
            left_over = count // distance
            radix = 2 if left_over.bit_length() % 2 == 0 else 4
            there = [
                lax.ppermute(sums, axis, [(i, i ^ (j * distance)) for i in range(count)]) for j in range(1, radix)
            ]
            sums = sums + there[0]
            if radix == 4:
                sums = sums + (there[1] + there[2])
            distance *= radix
    return sums


def shards(terminal, crowding, density, fractions, offsets, control_cost):
    height, breadth = terminal.shape
    count = breadth // LANES
    steps_count, controls = control_cost.shape
    cells = height * breadth * lax.axis_size("gx") * lax.axis_size("gy")
    table = shift_table(offsets, padded_rows(height))
    costs = time_step * control_cost.reshape(-1)
    inside, outside = tuple(range(1, count - 1)), (0, count - 1)

    def both_groups(tiles, halo, sides, entry, moment, backward, policy, which=0, sums=None):
        common = (entry, moment * controls, controls, moment, table, tiles, halo)
        inner, inner_edges, inner_rest = step(
            inside, *common, None, None, fractions, backward, None if policy is None else policy[0], which, None
        )
        outer, edges, outer_rest = step(
            outside,
            *common,
            sides,
            inner_edges,
            fractions,
            backward,
            None if policy is None else policy[1],
            which,
            None if policy is None else (sums, *inner_rest),
        )
        return [outer[0], *inner, outer[1]], edges, (inner_rest, outer_rest)

    (tiles, dense), edges = split(terminal, density)
    first_halo = row_halo(edges)
    halo = first_halo
    policies = [None] * steps_count
    for moment in reversed(range(steps_count)):
        if moment < steps_count - 1:
            halo = row_halo(edges)
        sides = column_halo(halo, tiles)
        entry = moment * controls * FIELDS
        tiles, edges, policies[moment] = both_groups(tiles, halo, sides, entry, moment, (costs, crowding), None)
    value = jnp.concatenate(tiles, axis=1)

    tiles, halo = dense, first_halo
    sums = jnp.zeros((SUBLANES, LANES), jnp.float32)
    for moment in range(steps_count):
        if moment > 0:
            halo = row_halo(edges)
        which = 0 if moment else 1
        sides = column_halo(halo, tiles, which)
        entry = (steps_count + moment) * controls * FIELDS
        tiles, edges, (_, (sums,)) = both_groups(
            tiles, halo, sides, entry, moment, None, policies[moment], which, sums
        )
    totals = everywhere(sums)[0, :steps_count] / cells
    masses = []
    scale = jnp.float32(1.0)
    for moment in range(steps_count):
        masses.append(totals[moment] / scale)
        scale = totals[moment] + epsilon * scale
    return (value, jnp.concatenate(tiles, axis=1) / scale, jnp.stack(masses))


def solution(mesh):
    return jax.shard_map(
        shards,
        mesh=mesh,
        in_specs=(P("gx", "gy"), P("gx", "gy"), P("gx", "gy"), P(None, None, "gx", "gy"), P(), P()),
        out_specs=(P("gx", "gy"), P("gx", "gy"), P()),
        check_vma=False,
    )
```
